32 devices in a mesh: rep: 4 (over y, core), ep: 8 (over z, x).
Axes of the slice: x: 2, y: 2, z: 4, core: 2. Of those that a mesh axis runs over, the one named last changes fastest.
Arguments:
- tokens: bfloat16 [4096, 1024], P(('rep', 'ep')), may hold values from -6 to 6
- expert_ids: int32 [4096, 8], P(('rep', 'ep')), may hold values from 0 to 15, all different within a row; in each aligned block of 128 rows (0 to 127, 128 to 255, ...) at most 96 rows name the same one
- route_weights: float32 [4096, 8], P(('rep', 'ep')), may hold values from 0.03 to 0.5
- out_grad: bfloat16 [4096, 1024], P(('rep', 'ep')), may hold values from -4 to 4
- gate_weight: bfloat16 [16, 1024, 384], P('ep'), may hold values from -0.1875 to 0.1875
- up_weight: bfloat16 [16, 1024, 384], P('ep'), may hold values from -0.1875 to 0.1875
- down_weight: bfloat16 [16, 384, 1024], P('ep'), may hold values from -0.3125 to 0.3125
Outputs:
- layer_out: bfloat16 [4096, 1024], P(('rep', 'ep'))
- token_grad: bfloat16 [4096, 1024], P(('rep', 'ep'))
- route_grad: float32 [4096, 8], P(('rep', 'ep'))
- gate_weight_grad: float32 [16, 1024, 384], P('ep', 'rep')
- up_weight_grad: float32 [16, 1024, 384], P('ep', 'rep')
- down_weight_grad: float32 [16, 384, 1024], P('ep', 'rep')
The draws below stay inside these ranges and needn't reach their ends.
Inputs may be any that keep to these rules, and one draw needn't show every extreme that they name: `expert_ids`: each row names 8 different experts. Among the rows of one device (an aligned block of 128 rows) no expert is named more than 96 times, and in every draw some expert is named exactly 96 times by the rows of some device.
All inputs are finite; a program needn't handle non-finite values.
Results may differ from the reference program's by a relative error of at most 0.014.
Values may be sent and summed in bfloat16 or wider, within the bound.
No kernel may reach another device: no remote copies, remote signals or barrier semaphores. Data moves between devices by JAX's collectives and lax.ppermute only.
A program may use at most 128 MiB of HBM per device.

```python
import math
import jax
import jax.numpy as jnp
import numpy as np
from jax import lax

D = 1024
FF = 384
TOP = 8
TOK_DEV = 128
EXPERTS = 16
TOKENS = 4096
CAP = 96
N_REP = 4
N_EP = 8


def level_of(rng, extent, shards, low, top_value):
    def one(dim, parts):
        draws = jax.random.uniform(jax.random.fold_in(jax.random.fold_in(rng, 6), dim), (parts,), jnp.float32, low / len(shards), top_value / len(shards))
        return jnp.repeat(jnp.exp(draws), extent[dim] // parts).reshape((-1,) + (1,) * (len(extent) - dim - 1))

    level = one(*shards[0])
    for cut in shards[1:]:
        level = level * one(*cut)
    return level


def shared_out(rng, own, number, rows, count, top, most, skew):
    sequence = jax.random.permutation(rng, count)
    packed, common = portions_of(count, rows * top, most, skew, True), portions_of(count, rows * top, most, skew, False)
    places = jnp.arange(count)

    def named(tallies, offset_by):
        used = int((tallies > 0).sum())
        fixed = max(1, used // 4)
        moved = fixed + (places - fixed + offset_by * (used - fixed)) % max(1, count - fixed)
        return jnp.zeros((count,), jnp.int32).at[sequence[jnp.where(places < fixed, places, moved)]].set(jnp.asarray(tallies, jnp.int32))

    tallies = jnp.where(number % 4 == 0, named(packed, number // 4), named(common, number - number // 4 - 1))
    mixed = jax.random.permutation(jax.random.fold_in(own, 3), count)
    donor, taker = mixed[0:count // 2 * 2:2], mixed[1:count // 2 * 2:2]
    slack = jnp.minimum(tallies[donor] - 1, most - tallies[taker]) // 2
    slack = jnp.where((donor == sequence[0]) | (taker == sequence[0]) | (tallies[taker] == 0), 0, jnp.maximum(slack, 0))
    moved = jax.random.randint(jax.random.fold_in(own, 4), (count // 2,), 0, 1 << 20) % (slack + 1)
    tallies = tallies.at[donor].add(-moved).at[taker].add(moved)
    labels = jnp.searchsorted(jnp.cumsum(tallies), jnp.arange(rows * top), side="right").astype(jnp.int32)
    table = labels.reshape(top, rows).T
    table = table[jax.random.permutation(jax.random.fold_in(own, 1), rows)]
    offset_by = jax.random.randint(jax.random.fold_in(own, 2), (rows, 1), 0, top)
    return jnp.take_along_axis(table, (jnp.arange(top)[None, :] + offset_by) % top, axis=1)


def portions_of(amount, total, limit, slope, full):
    loads = [(1 << 20) // math.isqrt(grade ** slope) + 1 for grade in range(1, amount + 1)]
    largest = limit if full else min(limit, max(-(-total // amount), total * loads[0] // sum(loads)))
    least = 1 if total - largest >= amount - 1 else 0
    counts, surplus = [largest] + [least] * (amount - 1), total - largest - least * (amount - 1)
    while surplus > 0:
        free = [i for i in range(1, amount) if counts[i] < largest] or [i for i in range(1, amount) if counts[i] < limit]
        mass, remaining = sum([loads[i] for i in free]), surplus
        for i in free:
            addition = min(limit - counts[i], max(1, remaining * loads[i] // mass), surplus)
            counts[i] = counts[i] + addition
            surplus = surplus - addition
    return np.array(counts)


def bell_draw(stream_key, dims, deviation, most, pieces=(), held_as=jnp.bfloat16):
    array = jax.random.normal(stream_key, dims, jnp.float32) * deviation
    if len(pieces) > 0:
        array = level_of(stream_key, dims, pieces, -0.22, 0.18) * array
    return jnp.clip(array, min=-most, max=most).astype(held_as)


def setup_inputs(seed: int = 0) -> dict:
    key_list = jax.random.split(jax.random.key(seed), 8)
    tokens = bell_draw(key_list[0], (TOKENS, D), 1.0, 6.0, ((0, 32),))
    expert_ids_keys = jax.random.split(jax.random.fold_in(key_list[1], 1), TOKENS // TOK_DEV)
    expert_ids_turns = jax.random.permutation(jax.random.fold_in(key_list[1], 3), TOKENS // TOK_DEV)
    expert_ids = jax.vmap(lambda own, number: shared_out(jax.random.fold_in(key_list[1], 2), own, number, TOK_DEV, EXPERTS, TOP, CAP, 1))(expert_ids_keys, expert_ids_turns).reshape((TOKENS, TOP))
    route_weights = jnp.clip(jnp.exp(math.log(0.5) - 2.8134107 * jax.random.uniform(key_list[2], (TOKENS, TOP), jnp.float32) ** level_of(key_list[2], (TOKENS, TOP), ((0, 32),), -0.2, 0.2)), 0.03, 0.5)
    out_grad = bell_draw(key_list[3], (TOKENS, D), 0.5, 4.0, ((0, 32),))
    gate_weight = bell_draw(key_list[4], (EXPERTS, D, FF), D ** -0.5, 0.1875, ((0, 8),))
    up_weight = bell_draw(key_list[5], (EXPERTS, D, FF), D ** -0.5, 0.1875, ((0, 8),))
    down_weight = bell_draw(key_list[6], (EXPERTS, FF, D), FF ** -0.5, 0.3125, ((0, 8),))
    return dict(tokens=tokens, expert_ids=expert_ids, route_weights=route_weights, out_grad=out_grad, gate_weight=gate_weight, up_weight=up_weight, down_weight=down_weight)


def silu_parts(gate_pre):
    sigmoid_gate = jax.nn.sigmoid(gate_pre)
    return gate_pre * sigmoid_gate, sigmoid_gate * (1.0 + gate_pre * (1.0 - sigmoid_gate))


def replica_sum(left, right):
    left_parts = left.reshape(N_REP, N_EP * CAP, left.shape[1]).astype(jnp.float32)
    right_parts = right.reshape(N_REP, N_EP * CAP, right.shape[1]).astype(jnp.float32)
    partial_sums = jnp.einsum("rna,rnb->rab", left_parts, right_parts)
    return jnp.sum(partial_sums.astype(jnp.bfloat16).astype(jnp.float32), axis=0)


def reference(tokens, expert_ids, route_weights, out_grad, gate_weight, up_weight, down_weight):
    devices_all = N_REP * N_EP
    pair_total = TOKENS * TOP
    per_block = TOK_DEV * TOP
    block_ids = expert_ids.reshape(devices_all, per_block).astype(jnp.int32)
    columns = jnp.arange(EXPERTS, dtype=jnp.int32)
    onehot = (block_ids[:, :, None] == columns[None, None, :]).astype(jnp.int32)
    slot_rank = jnp.sum((jnp.cumsum(onehot, axis=1).astype(jnp.int32) - 1) * onehot, axis=2).astype(jnp.int32)
    block_base = (jnp.arange(devices_all, dtype=jnp.int32) * CAP)[:, None]
    position = (block_ids * (devices_all * CAP) + block_base + slot_rank).reshape(-1).astype(jnp.int32)
    table = jnp.full((EXPERTS * devices_all * CAP,), pair_total, jnp.int32)
    table = table.at[position].set(jnp.arange(pair_total, dtype=jnp.int32)).reshape(EXPERTS, devices_all * CAP)
    flat_weights = route_weights.reshape(-1)
    zero_half = jnp.zeros((), jnp.bfloat16)

    def per_expert(totals, inputs):
        slot_pairs, gate_matrix, up_matrix, down_matrix = inputs
        occupied = slot_pairs < pair_total
        pair_index = jnp.where(occupied, slot_pairs, 0).astype(jnp.int32)
        token_index = (pair_index // TOP).astype(jnp.int32)
        row_mask = occupied[:, None]
        weight_col = jnp.where(occupied, flat_weights[pair_index], 0.0)
        expert_in = jnp.where(row_mask, tokens[token_index], zero_half)
        grad_rows = out_grad[token_index]
        out_rows = jnp.where(row_mask, (weight_col[:, None] * grad_rows).astype(jnp.bfloat16), zero_half)
        gate_pre = jnp.dot(expert_in, gate_matrix, preferred_element_type=jnp.float32)
        up_pre = jnp.dot(expert_in, up_matrix, preferred_element_type=jnp.float32)
        silu_gate, silu_slope = silu_parts(gate_pre)
        hidden = (silu_gate * up_pre).astype(jnp.bfloat16)
        expert_out = jnp.dot(hidden, down_matrix, preferred_element_type=jnp.float32).astype(jnp.bfloat16)
        hidden_grad = jnp.dot(out_rows, down_matrix.T, preferred_element_type=jnp.float32)
        gate_delta = (hidden_grad * up_pre * silu_slope).astype(jnp.bfloat16)
        up_delta = (hidden_grad * silu_gate).astype(jnp.bfloat16)
        in_grads = (jnp.dot(gate_delta, gate_matrix.T, preferred_element_type=jnp.float32)
                    + jnp.dot(up_delta, up_matrix.T, preferred_element_type=jnp.float32)).astype(jnp.bfloat16)
        grad_gate = replica_sum(expert_in, gate_delta)
        grad_up = replica_sum(expert_in, up_delta)
        grad_down = replica_sum(hidden, out_rows)
        layer_total, input_total, route_total = totals
        layer_total = layer_total.at[token_index].add(weight_col[:, None] * expert_out.astype(jnp.float32))
        input_total = input_total.at[token_index].add(jnp.where(row_mask, in_grads.astype(jnp.float32), 0.0))
        route_terms = jnp.sum(grad_rows.astype(jnp.float32) * expert_out.astype(jnp.float32), axis=1)
        route_total = route_total.at[pair_index].add(jnp.where(occupied, route_terms, 0.0))
        return (layer_total, input_total, route_total), (grad_gate, grad_up, grad_down)

    start = (jnp.zeros((TOKENS, D), jnp.float32), jnp.zeros((TOKENS, D), jnp.float32),
             jnp.zeros((pair_total,), jnp.float32))
    totals, grads = lax.scan(per_expert, start, (table, gate_weight, up_weight, down_weight))
    layer_total, input_total, route_total = totals
    return (layer_total.astype(jnp.bfloat16), input_total.astype(jnp.bfloat16),
            route_total.reshape(TOKENS, TOP), grads[0], grads[1], grads[2])
```

```python
import functools

import jax
import jax.numpy as jnp
from jax import lax
from jax.experimental import pallas as pl
from jax.experimental.pallas import tpu as pltpu
from jax.sharding import PartitionSpec as P


NT = (((1,), (1,)), ((), ()))
TN = (((0,), (0,)), ((), ()))


def block_kernel(count, src_ref, *refs):
    blocks = refs[:count]
    w_ref, wg_ref, wu_ref, wd_ref = refs[count : count + 4]
    out_refs = refs[count + 4 : count + 4 + count]
    delta_ref, wh_ref, rg_ref = refs[count + 4 + count :]
    rows = blocks[0].shape[0] // 2
    local = wg_ref.shape[0]
    hidden_width = wg_ref.shape[2]
    x = jnp.concatenate([b[:rows, :] for b in blocks], axis=0)
    g = jnp.concatenate([b[rows:, :] for b in blocks], axis=0)
    w = jnp.concatenate([w_ref[src_ref[i]] for i in range(count)], axis=0)
    lane = lax.broadcasted_iota(jnp.int32, (count * rows, 128), 1)
    rg_all = jnp.zeros((count * rows, 128), jnp.float32)
    out = None
    grad = None
    for e in range(local):
        gate = jnp.dot(x, wg_ref[e], preferred_element_type=jnp.float32)
        up = jnp.dot(x, wu_ref[e], preferred_element_type=jnp.float32)
        s = jax.nn.sigmoid(gate)
        silu = gate * s
        hidden = silu * up
        we = w[:, e : e + 1]
        wh = (we * hidden).astype(jnp.bfloat16)
        hg = lax.dot_general(g, wd_ref[e], NT, preferred_element_type=jnp.float32)
        rg = jnp.sum(hidden * hg, axis=1, keepdims=True)
        rg_all = jnp.where(lane == e, rg, rg_all)
        hg = we * hg
        gd = (hg * up * (s * (1.0 + gate * (1.0 - s)))).astype(jnp.bfloat16)
        ud = (hg * silu).astype(jnp.bfloat16)
        delta_ref[:, e * hidden_width : (e + 1) * hidden_width] = gd
        delta_ref[:, (local + e) * hidden_width : (local + e + 1) * hidden_width] = ud
        wh_ref[:, e * hidden_width : (e + 1) * hidden_width] = wh
        o = jnp.dot(wh, wd_ref[e], preferred_element_type=jnp.float32)
        d = lax.dot_general(gd, wg_ref[e], NT, preferred_element_type=jnp.float32)
        d += lax.dot_general(ud, wu_ref[e], NT, preferred_element_type=jnp.float32)
        out = o if out is None else out + o
        grad = d if grad is None else grad + d
    for i in range(count):
        part = slice(i * rows, (i + 1) * rows)
        out_refs[i][:rows, :] = out[part].astype(jnp.bfloat16)
        out_refs[i][rows:, :] = grad[part].astype(jnp.bfloat16)
        rg_ref[i] = rg_all[part]


def run_blocks(blocks, sources, w_all, wg, wu, wd):
    count = len(blocks)
    rows2, width = blocks[0].shape
    rows = rows2 // 2
    local, _, hidden_width = wg.shape
    vmem = pl.BlockSpec(memory_space=pltpu.VMEM)
    return pl.pallas_call(
        functools.partial(block_kernel, count),
        out_shape=tuple(jax.ShapeDtypeStruct((rows2, width), jnp.bfloat16) for _ in blocks)
        + (
            jax.ShapeDtypeStruct((count * rows, 2 * local * hidden_width), jnp.bfloat16),
            jax.ShapeDtypeStruct((count * rows, local * hidden_width), jnp.bfloat16),
            jax.ShapeDtypeStruct((count, rows, 128), jnp.float32),
        ),
        in_specs=[pl.BlockSpec(memory_space=pltpu.SMEM)] + [vmem] * (count + 4),
        out_specs=tuple([vmem] * (count + 3)),
        compiler_params=pltpu.CompilerParams(vmem_limit_bytes=48 * 2**20),
        name="experts",
    )(sources, *blocks, w_all, wg, wu, wd)


def weight_kernel(groups, per, half, local, tr_ref, *refs):
    n = groups * per
    xs = refs[:n]
    gs = refs[n : 2 * n]
    deltas = refs[2 * n : 2 * n + groups]
    whs = refs[2 * n + groups : 2 * n + 2 * groups]
    send_in, send_down, keep_in, keep_down, scratch = refs[2 * n + 2 * groups :]
    j = pl.program_id(0)
    band = send_down.shape[1] // local

    @pl.when(j == 0)
    def _():
        total = None
        for k in range(groups):
            g = jnp.concatenate([gs[k * per + i][...] for i in range(per)], axis=0)
            part = lax.dot_general(whs[k][...], g, TN, preferred_element_type=jnp.float32)
            total = part if total is None else total + part
        scratch[...] = total

    total = None
    for k in range(groups):
        x = jnp.concatenate([xs[k * per + i][...] for i in range(per)], axis=0)
        part = lax.dot_general(x, deltas[k][...], TN, preferred_element_type=jnp.float32)
        total = part if total is None else total + part
    hidden_width = scratch.shape[0] // local
    down = []
    for e in range(local):
        start = pl.multiple_of(e * hidden_width + tr_ref[j] * band, 8)
        down.append(scratch[pl.ds(start, band), :])
    down = jnp.concatenate(down, axis=0)

    @pl.when(j < half)
    def _():
        send_in[0] = total.astype(jnp.bfloat16)
        send_down[0] = down.astype(jnp.bfloat16)

    @pl.when(j >= half)
    def _():
        keep_in[0] = total
        keep_down[0] = down


def weight_grads(blocks, deltas, whs, targets, half, local):
    groups = len(deltas)
    per = len(blocks) // groups
    rows2, width = blocks[0].shape
    rows = rows2 // 2
    n_rep = 2 * half
    depth = width // n_rep
    in_width = deltas[0].shape[1]
    down_rows = whs[0].shape[1]
    band = down_rows // n_rep
    f = functools.partial(weight_kernel, groups, per, half, local)
    first = lambda j, tr: (jnp.minimum(j, half - 1), 0, 0)
    last = lambda j, tr: (jnp.maximum(j - half, 0), 0, 0)
    return pl.pallas_call(
        f,
        out_shape=(
            jax.ShapeDtypeStruct((half, depth, in_width), jnp.bfloat16),
            jax.ShapeDtypeStruct((half, band, width), jnp.bfloat16),
            jax.ShapeDtypeStruct((half, depth, in_width), jnp.float32),
            jax.ShapeDtypeStruct((half, band, width), jnp.float32),
        ),
        grid_spec=pltpu.PrefetchScalarGridSpec(
            num_scalar_prefetch=1,
            grid=(n_rep,),
            in_specs=[pl.BlockSpec((rows, depth), lambda j, tr: (0, tr[j])) for _ in blocks]
            + [pl.BlockSpec((rows, width), lambda j, tr: (1, 0)) for _ in blocks]
            + [pl.BlockSpec(d.shape, lambda j, tr: (0, 0)) for d in deltas]
            + [pl.BlockSpec(h.shape, lambda j, tr: (0, 0)) for h in whs],
            out_specs=(
                pl.BlockSpec((1, depth, in_width), first),
                pl.BlockSpec((1, band, width), first),
                pl.BlockSpec((1, depth, in_width), last),
                pl.BlockSpec((1, band, width), last),
            ),
            scratch_shapes=[pltpu.VMEM((down_rows, width), jnp.float32)],
        ),
        compiler_params=pltpu.CompilerParams(vmem_limit_bytes=56 * 2**20),
        name="weights",
    )(targets, *blocks, *blocks, *deltas, *whs)


def per_device(tokens, expert_ids, route_weights, out_grad, wg, wu, wd):
    rows, width = tokens.shape
    local, _, hidden_width = wg.shape
    n_ep = lax.axis_size("ep")
    n_rep = lax.axis_size("rep")
    experts = local * n_ep
    fast = 2 if n_ep % 2 == 0 else 1
    slow = n_ep // fast
    here = lax.axis_index("ep")
    a, b = here // fast, here % fast

    def shift_slow(v, s):
        pairs = [(i * fast + j, (i + s) % slow * fast + j) for i in range(slow) for j in range(fast)]
        return lax.ppermute(v, "ep", pairs)

    def shift_fast(v, t):
        pairs = [(i * fast + j, i * fast + (j + t) % fast) for i in range(slow) for j in range(fast)]
        return lax.ppermute(v, "ep", pairs)

    order = [0] + sorted(range(1, slow), key=lambda s: -min(s, slow - s))
    mine = jnp.concatenate([tokens, out_grad], axis=0)

    ids_t = expert_ids.T
    weights_t = route_weights.T
    named = ids_t[None, :, :] == jnp.arange(experts, dtype=jnp.int32)[:, None, None]
    dense = jnp.sum(jnp.where(named, weights_t[None, :, :], 0.0), axis=1)
    w_all = lax.all_to_all(
        dense.reshape(n_ep, local, rows), "ep", split_axis=0, concat_axis=0, tiled=True
    )
    w_all = jnp.swapaxes(w_all, 1, 2)

    gathered = {0: mine}
    for s in order[1:]:
        gathered[s] = shift_slow(mine, s)
    blocks, deltas, whs, rgs, sources = {}, {}, {}, {}, {}
    kept, arriving = {}, {}
    for s in order:
        group = [gathered[s]] + [shift_fast(gathered[s], t) for t in range(1, fast)]
        src = [(a - s) % slow * fast + (b - t) % fast for t in range(fast)]
        sources[s] = src
        result = run_blocks(group, jnp.stack(src).astype(jnp.int32), w_all, wg, wu, wd)
        blocks[s] = group
        deltas[s], whs[s], rgs[s] = result[fast:]
        kept[s] = result[0]
        arriving[s] = [shift_fast(result[t], -t) for t in range(1, fast)]
    final = None
    for s in order[1:] + [0]:
        q = kept[s].astype(jnp.float32)
        for r in arriving[s]:
            q = q + r.astype(jnp.float32)
        if s:
            q = shift_slow(q.astype(jnp.bfloat16), -s).astype(jnp.float32)
        final = q if final is None else final + q
    layer_out = final[:rows].astype(jnp.bfloat16)
    token_grad = final[rows:].astype(jnp.bfloat16)

    rel = jnp.concatenate([rgs[s][:, :, :local] for s in order], axis=0)
    where = jnp.stack([i for s in order for i in sources[s]])
    back = jnp.swapaxes(rel, 1, 2)
    onehot = (where[None, :] == jnp.arange(n_ep)[:, None]).astype(jnp.float32)
    back = jnp.sum(onehot[:, :, None, None] * back[None], axis=1)
    back = lax.all_to_all(back, "ep", split_axis=0, concat_axis=0, tiled=True)
    back = back.reshape(experts, rows)
    route_grad = jnp.sum(jnp.where(named, back[:, None, :], 0.0), axis=0).T

    r = lax.axis_index("rep")
    half = n_rep // 2
    y, c = r // 2, r % 2
    targets = jnp.stack(
        [(y + dy) % half * 2 + (c + dc) % 2 for dc in (1, 0) for dy in range(half)]
    ).astype(jnp.int32)
    send_in, send_down, keep_in, keep_down = weight_grads(
        [v for s in order for v in blocks[s]],
        [deltas[s] for s in order],
        [whs[s] for s in order],
        targets,
        half,
        local,
    )
    core_pairs = [(i, i ^ 1) for i in range(n_rep)]

    def rep_sum(send, keep):
        got = lax.ppermute(send, "rep", core_pairs)
        total = keep + got.astype(jnp.float32)
        share = total[0]
        for dy in range(1, half):
            pairs = [(i, (i // 2 + dy) % half * 2 + i % 2) for i in range(n_rep)]
            share = share + lax.ppermute(total[dy].astype(jnp.bfloat16), "rep", pairs).astype(jnp.float32)
        return share

    share_in = rep_sum(send_in, keep_in)
    share_down = rep_sum(send_down, keep_down)
    cut = [share_in[:, i * hidden_width : (i + 1) * hidden_width] for i in range(2 * local)]
    gate_share = jnp.stack(cut[:local])
    up_share = jnp.stack(cut[local:])
    down_share = share_down.reshape(local, hidden_width // n_rep, width)
    return (layer_out, token_grad, route_grad, gate_share, up_share, down_share)


def solution(mesh):
    return jax.shard_map(
        per_device,
        mesh=mesh,
        in_specs=(
            P(("rep", "ep"), None),
            P(("rep", "ep"), None),
            P(("rep", "ep"), None),
            P(("rep", "ep"), None),
            P("ep", None, None),
            P("ep", None, None),
            P("ep", None, None),
        ),
        out_specs=(
            P(("rep", "ep"), None),
            P(("rep", "ep"), None),
            P(("rep", "ep"), None),
            P("ep", "rep", None),
            P("ep", "rep", None),
            P("ep", "rep", None),
        ),
        check_vma=False,
    )
```

```python
import functools

import jax
import jax.numpy as jnp
from jax import lax
from jax.experimental import pallas as pl
from jax.experimental.pallas import tpu as pltpu
from jax.sharding import PartitionSpec as P


NT = (((1,), (1,)), ((), ()))
TN = (((0,), (0,)), ((), ()))


def in_hbm(value):
    return pltpu.with_memory_space_constraint(value, pltpu.HBM)


def block_kernel(count, src_ref, w_ref, *refs):
    blocks = refs[:count]
    wg_hbm, wu_hbm, wd_hbm = refs[count : count + 3]
    outs = refs[count + 3 : 2 * count + 3]
    delta_hbm, wh_hbm, rg_ref = refs[2 * count + 3 : 2 * count + 6]
    x_ref, g_ref, wg_ref, wu_ref, wd_ref, o_ref, delta_ref, wh_ref, sem, out_sem = refs[2 * count + 6 :]
    rows = blocks[0].shape[0] // 2
    local, _, hidden_width = wg_ref.shape
    copies = {}

    def fetch(key, slot, source, target):
        copies[key] = pltpu.make_async_copy(source, target, sem.at[slot])
        copies[key].start()

    for i in range(count):
        fetch(("x", i), i, blocks[i].at[pl.ds(0, rows)], x_ref.at[pl.ds(i * rows, rows)])
    for e in range(local):
        base = 2 * count + 3 * e
        fetch(("wg", e), base, wg_hbm.at[e], wg_ref.at[e])
        fetch(("wu", e), base + 1, wu_hbm.at[e], wu_ref.at[e])
        if e == 0:
            for i in range(count):
                fetch(
                    ("g", i),
                    count + i,
                    blocks[i].at[pl.ds(rows, rows)],
                    g_ref.at[pl.ds(i * rows, rows)],
                )
        fetch(("wd", e), base + 2, wd_hbm.at[e], wd_ref.at[e])
    columns = [
        [jnp.broadcast_to(w_ref[src_ref[i], e : e + 1, :], (128, rows)).T for i in range(count)]
        for e in range(local)
    ]
    lane = lax.broadcasted_iota(jnp.int32, (count * rows, 128), 1)
    rg_all = jnp.zeros((count * rows, 128), jnp.float32)
    for i in range(count):
        copies["x", i].wait()
    x = x_ref[...]
    g = None
    out = None
    grad = None
    stores = []
    for e in range(local):
        copies["wg", e].wait()
        gate = jnp.dot(x, wg_ref[e], preferred_element_type=jnp.float32)
        copies["wu", e].wait()
        up = jnp.dot(x, wu_ref[e], preferred_element_type=jnp.float32)
        s = jax.nn.sigmoid(gate)
        silu = gate * s
        hidden = silu * up
        we = jnp.concatenate(columns[e], axis=0)[:, :1]
        wh = (we * hidden).astype(jnp.bfloat16)
        if e == 0:
            for i in range(count):
                copies["g", i].wait()
            g = g_ref[...]
        copies["wd", e].wait()
        hg = lax.dot_general(g, wd_ref[e], NT, preferred_element_type=jnp.float32)
        rg = jnp.sum(hidden * hg, axis=1, keepdims=True)
        rg_all = jnp.where(lane == e, rg, rg_all)
        hg = we * hg
        gd = (hg * up * (s * (1.0 + gate * (1.0 - s)))).astype(jnp.bfloat16)
        ud = (hg * silu).astype(jnp.bfloat16)
        delta_ref[:, e * hidden_width : (e + 1) * hidden_width] = gd
        delta_ref[:, (local + e) * hidden_width : (local + e + 1) * hidden_width] = ud
        wh_ref[:, e * hidden_width : (e + 1) * hidden_width] = wh
        if e == local - 1:
            stores.append(pltpu.make_async_copy(delta_ref, delta_hbm, out_sem.at[0]))
            stores.append(pltpu.make_async_copy(wh_ref, wh_hbm, out_sem.at[1]))
            stores[0].start()
            stores[1].start()
        o = jnp.dot(wh, wd_ref[e], preferred_element_type=jnp.float32)
        d = lax.dot_general(gd, wg_ref[e], NT, preferred_element_type=jnp.float32)
        d += lax.dot_general(ud, wu_ref[e], NT, preferred_element_type=jnp.float32)
        out = o if out is None else out + o
        grad = d if grad is None else grad + d
    for i in reversed(range(count)):
        part = slice(i * rows, (i + 1) * rows)
        o_ref[i, :rows, :] = out[part].astype(jnp.bfloat16)
        o_ref[i, rows:, :] = grad[part].astype(jnp.bfloat16)
        stores.append(pltpu.make_async_copy(o_ref.at[i], outs[i], out_sem.at[2 + i]))
        stores[-1].start()
    for i in range(count):
        rg_ref[i] = rg_all[i * rows : (i + 1) * rows].T[:local]
    for copy in stores:
        copy.wait()


def run_blocks(blocks, sources, w_all, wg, wu, wd):
    count = len(blocks)
    rows2, width = blocks[0].shape
    rows = rows2 // 2
    local, _, hidden_width = wg.shape
    vmem = pl.BlockSpec(memory_space=pltpu.VMEM)
    hbm = pl.BlockSpec(memory_space=pltpu.HBM)
    bf16 = jnp.bfloat16
    return pl.pallas_call(
        functools.partial(block_kernel, count),
        out_shape=tuple(pltpu.HBM((rows2, width), bf16) for _ in blocks)
        + (
            pltpu.HBM((count * rows, 2 * local * hidden_width), bf16),
            pltpu.HBM((count * rows, local * hidden_width), bf16),
            jax.ShapeDtypeStruct((count, local, rows), jnp.float32),
        ),
        in_specs=[pl.BlockSpec(memory_space=pltpu.SMEM), vmem]
        + [pl.BlockSpec(memory_space=pl.ANY)] * count
        + [hbm] * 3,
        out_specs=tuple([hbm] * (count + 2) + [vmem]),
        scratch_shapes=[
            pltpu.VMEM((count * rows, width), bf16),
            pltpu.VMEM((count * rows, width), bf16),
            pltpu.VMEM(wg.shape, bf16),
            pltpu.VMEM(wu.shape, bf16),
            pltpu.VMEM(wd.shape, bf16),
            pltpu.VMEM((count, rows2, width), bf16),
            pltpu.VMEM((count * rows, 2 * local * hidden_width), bf16),
            pltpu.VMEM((count * rows, local * hidden_width), bf16),
            pltpu.SemaphoreType.DMA((2 * count + 3 * local,)),
            pltpu.SemaphoreType.DMA((2 + count,)),
        ],
        compiler_params=pltpu.CompilerParams(vmem_limit_bytes=24 * 2**20),
        name="experts",
    )(sources, w_all, *blocks, in_hbm(wg), in_hbm(wu), in_hbm(wd))


def weight_kernel(groups, per, half, local, tr_ref, *refs):
    n = groups * per
    xs = refs[:n]
    gs = refs[n : 2 * n]
    deltas = refs[2 * n : 2 * n + groups]
    whs = refs[2 * n + groups : 2 * n + 2 * groups]
    send_in, send_down, keep_in, keep_down, scratch = refs[2 * n + 2 * groups :]
    j = pl.program_id(0)
    band = send_down.shape[1] // local

    @pl.when(j == 0)
    def _():
        total = None
        for k in range(groups):
            g = jnp.concatenate([gs[k * per + i][...] for i in range(per)], axis=0)
            part = lax.dot_general(whs[k][...], g, TN, preferred_element_type=jnp.float32)
            total = part if total is None else total + part
        scratch[...] = total

    total = None
    for k in range(groups):
        x = jnp.concatenate([xs[k * per + i][...] for i in range(per)], axis=0)
        part = lax.dot_general(x, deltas[k][...], TN, preferred_element_type=jnp.float32)
        total = part if total is None else total + part
    hidden_width = scratch.shape[0] // local
    down = []
    for e in range(local):
        start = pl.multiple_of(e * hidden_width + tr_ref[j] * band, 8)
        down.append(scratch[pl.ds(start, band), :])
    down = jnp.concatenate(down, axis=0)

    @pl.when(j < half)
    def _():
        send_in[0] = total.astype(jnp.bfloat16)
        send_down[0] = down.astype(jnp.bfloat16)

    @pl.when(j >= half)
    def _():
        keep_in[0] = total
        keep_down[0] = down


def weight_grads(blocks, deltas, whs, targets, half, local):
    groups = len(deltas)
    per = len(blocks) // groups
    rows2, width = blocks[0].shape
    rows = rows2 // 2
    n_rep = 2 * half
    depth = width // n_rep
    in_width = deltas[0].shape[1]
    down_rows = whs[0].shape[1]
    band = down_rows // n_rep
    f = functools.partial(weight_kernel, groups, per, half, local)
    first = lambda j, tr: (jnp.minimum(j, half - 1), 0, 0)
    last = lambda j, tr: (jnp.maximum(j - half, 0), 0, 0)
    return pl.pallas_call(
        f,
        out_shape=(
            jax.ShapeDtypeStruct((half, depth, in_width), jnp.bfloat16),
            jax.ShapeDtypeStruct((half, band, width), jnp.bfloat16),
            jax.ShapeDtypeStruct((half, depth, in_width), jnp.float32),
            jax.ShapeDtypeStruct((half, band, width), jnp.float32),
        ),
        grid_spec=pltpu.PrefetchScalarGridSpec(
            num_scalar_prefetch=1,
            grid=(n_rep,),
            in_specs=[pl.BlockSpec((rows, depth), lambda j, tr: (0, tr[j])) for _ in blocks]
            + [pl.BlockSpec((rows, width), lambda j, tr: (1, 0)) for _ in blocks]
            + [pl.BlockSpec(d.shape, lambda j, tr: (0, 0)) for d in deltas]
            + [pl.BlockSpec(h.shape, lambda j, tr: (0, 0)) for h in whs],
            out_specs=(
                pl.BlockSpec((1, depth, in_width), first),
                pl.BlockSpec((1, band, width), first),
                pl.BlockSpec((1, depth, in_width), last),
                pl.BlockSpec((1, band, width), last),
            ),
            scratch_shapes=[pltpu.VMEM((down_rows, width), jnp.float32)],
        ),
        compiler_params=pltpu.CompilerParams(vmem_limit_bytes=36 * 2**20),
        name="weights",
    )(targets, *blocks, *blocks, *[in_hbm(v) for v in deltas], *[in_hbm(v) for v in whs])


def after(value, *first):
    return lax.optimization_barrier((value,) + first)[0]


def per_device(tokens, expert_ids, route_weights, out_grad, wg, wu, wd):
    rows, width = tokens.shape
    local, _, hidden_width = wg.shape
    n_ep = lax.axis_size("ep")
    n_rep = lax.axis_size("rep")
    experts = local * n_ep
    fast = 2 if n_ep % 2 == 0 else 1
    slow = n_ep // fast
    here = lax.axis_index("ep")
    a, b = here // fast, here % fast

    def swap_slow(v, bit):
        pairs = [(i * fast + j, (i ^ bit) * fast + j) for i in range(slow) for j in range(fast)]
        return lax.ppermute(v, "ep", pairs)

    def shift_fast(v, t):
        pairs = [(i * fast + j, i * fast + (j + t) % fast) for i in range(slow) for j in range(fast)]
        return lax.ppermute(v, "ep", pairs)

    mine = jnp.concatenate([tokens, out_grad], axis=0)

    ids_t = expert_ids.T
    weights_t = route_weights.T
    named = ids_t[None, :, :] == jnp.arange(experts, dtype=jnp.int32)[:, None, None]
    dense = jnp.sum(jnp.where(named, weights_t[None, :, :], 0.0), axis=1)
    w_all = lax.all_to_all(
        dense.reshape(n_ep, local, rows), "ep", split_axis=0, concat_axis=0, tiled=True
    )

    bits = [1 << i for i in range(slow.bit_length() - 1)]
    gathered = {0: mine}
    sources = {}
    forwarded = {}
    blocks, deltas, whs, rgs = {}, {}, {}, {}
    kept, leaving = {}, {}
    order = list(range(slow))

    def forward(d):
        forwarded[d] = [shift_fast(gathered[d], t) for t in range(1, fast)]

    def compute(d):
        src = [(a ^ d) * fast + (b - t) % fast for t in range(fast)]
        sources[d] = src
        group = [gathered[d]] + forwarded[d]
        result = run_blocks(group, jnp.stack(src).astype(jnp.int32), w_all, wg, wu, wd)
        blocks[d] = group
        deltas[d], whs[d], rgs[d] = result[fast:]
        kept[d] = result[0]
        leaving[d] = result[1:fast]

    forward(0)
    if slow == 4:
        gathered[1] = swap_slow(mine, 1)
        gathered[2] = swap_slow(mine, 2)
        forward(1)
        gathered[0] = after(gathered[0], gathered[1])
        compute(0)
        gathered[2] = after(gathered[2], kept[0])
        forward(2)
        gathered[3] = swap_slow(gathered[2], 1)
        gathered[1] = after(gathered[1], gathered[2])
        compute(1)
        gathered[3] = after(gathered[3], kept[1])
        forward(3)
        gathered[2] = after(gathered[2], gathered[3])
        compute(2)
        gathered[3] = after(gathered[3], kept[2])
        compute(3)
    else:
        for bit in reversed(bits):
            for d in list(gathered):
                gathered[d | bit] = swap_slow(gathered[d], bit)
        for d in order:
            if d:
                forward(d)
            compute(d)
    last = order[-1]
    arriving = {}
    for d in reversed(order):
        sent = [v if d == last else after(v, kept[last]) for v in leaving[d]]
        arriving[d] = [shift_fast(v, -t - 1) for t, v in enumerate(sent)]
    total = {}
    for d in reversed(order):
        total[d] = kept[d].astype(jnp.float32)
        for v in arriving[d]:
            total[d] = total[d] + v.astype(jnp.float32)
    for bit in bits:
        for d in reversed([d for d in total if d & bit]):
            got = swap_slow(total.pop(d).astype(jnp.bfloat16), bit)
            total[d ^ bit] = total[d ^ bit] + got.astype(jnp.float32)
    final = total[0]
    layer_out = final[:rows].astype(jnp.bfloat16)
    token_grad = final[rows:].astype(jnp.bfloat16)

    rel = jnp.concatenate([rgs[s] for s in order], axis=0)
    where = jnp.stack([i for s in order for i in sources[s]])
    onehot = (where[None, :] == jnp.arange(n_ep)[:, None]).astype(jnp.float32)
    back = jnp.sum(onehot[:, :, None, None] * rel[None], axis=1)
    back = lax.all_to_all(back, "ep", split_axis=0, concat_axis=0, tiled=True)
    back = back.reshape(experts, rows)
    route_grad = jnp.sum(jnp.where(named, back[:, None, :], 0.0), axis=0).T

    r = lax.axis_index("rep")
    half = n_rep // 2
    y, c = r // 2, r % 2
    targets = jnp.stack(
        [(y + dy) % half * 2 + (c + dc) % 2 for dc in (1, 0) for dy in range(half)]
    ).astype(jnp.int32)
    send_in, send_down, keep_in, keep_down = weight_grads(
        [v for s in order for v in blocks[s]],
        [deltas[s] for s in order],
        [whs[s] for s in order],
        targets,
        half,
        local,
    )
    core_pairs = [(i, i ^ 1) for i in range(n_rep)]

    def rep_sum(send, keep):
        got = lax.ppermute(send, "rep", core_pairs)
        total = keep + got.astype(jnp.float32)
        share = total[0]
        for dy in range(1, half):
            pairs = [(i, (i // 2 + dy) % half * 2 + i % 2) for i in range(n_rep)]
            share = share + lax.ppermute(total[dy].astype(jnp.bfloat16), "rep", pairs).astype(jnp.float32)
        return share

    share_in = rep_sum(send_in, keep_in)
    share_down = rep_sum(send_down, keep_down)
    cut = [share_in[:, i * hidden_width : (i + 1) * hidden_width] for i in range(2 * local)]
    gate_share = jnp.stack(cut[:local])
    up_share = jnp.stack(cut[local:])
    down_share = share_down.reshape(local, hidden_width // n_rep, width)
    return (layer_out, token_grad, route_grad, gate_share, up_share, down_share)


def solution(mesh):
    return jax.shard_map(
        per_device,
        mesh=mesh,
        in_specs=(
            P(("rep", "ep"), None),
            P(("rep", "ep"), None),
            P(("rep", "ep"), None),
            P(("rep", "ep"), None),
            P("ep", None, None),
            P("ep", None, None),
            P("ep", None, None),
        ),
        out_specs=(
            P(("rep", "ep"), None),
            P(("rep", "ep"), None),
            P(("rep", "ep"), None),
            P("ep", "rep", None),
            P("ep", "rep", None),
            P("ep", "rep", None),
        ),
        check_vma=False,
    )
```
